512 devices in a mesh: pipe: 8 (over x, core), fsdp: 32 (over y, z_lo), rep: 2 (over z_hi).
Axes of the slice: x: 4, y: 8, z: 8 (z_hi: 2, z_lo: 4; z = z_hi * 4 + z_lo), core: 2. Of those that a mesh axis runs over, the one named last changes fastest.
Arguments:
- section_acts: bfloat16 [8, 2, 4096, 3072], P('pipe', 'rep', 'fsdp'), may hold values from -6 to 6
- route_ids: int32 [8, 2, 4096, 2], P('pipe', 'rep', 'fsdp'), may hold values from 0 to 7, as said below
- gate_weight: bfloat16 [8, 3072, 8192], P('pipe', None, 'fsdp'), may hold values from -0.109375 to 0.109375
- hidden_cot: bfloat16 [8, 2, 768, 8192], P('pipe', 'rep', None, 'fsdp'), may hold values from -6 to 6
Outputs:
- weight_grad: bfloat16 [8, 3072, 8192], P('pipe', 'rep', 'fsdp')
- acts_grad: bfloat16 [8, 2, 4096, 3072], P('pipe', 'rep', 'fsdp')
The draws below stay inside these ranges and needn't reach their ends.
Inputs may be any that keep to these rules, and one draw needn't show every extreme that they name: `route_ids`: in every section, replica and block of 128 consecutive tokens at most 24 tokens name expert 0, and in every section and replica some block has exactly 24; a token's two ids differ.
All inputs are finite; a program needn't handle non-finite values.
Results may differ from the reference program's by a relative error of at most 0.0059.
Values may be sent and summed in bfloat16 or wider, within the bound.
No kernel may reach another device: no remote copies, remote signals or barrier semaphores. Data moves between devices by JAX's collectives and lax.ppermute only.
A program may use at most 128 MiB of HBM per device.

```python
import jax
import jax.numpy as jnp

D = 3072
FF = 8192
EXPERTS = 8
TOPK = 2
TOK_DEV = 128
CAP = 24
SECTIONS = 8
REPLICAS = 2
TOKENS = 4096
SLOTS = 768


def draw_route_ids(key, part):
    subkeys = jax.random.split(jax.random.fold_in(key, 17), 6)
    blocks = TOKENS // TOK_DEV
    levels_table = jnp.array([CAP, CAP // 2, CAP // 3, CAP // 4], jnp.int32)
    levels = jax.random.randint(subkeys[0], (SECTIONS, REPLICAS, blocks), 0, 4)
    counts = levels_table[levels]
    chosen = jax.random.randint(subkeys[1], (SECTIONS, REPLICAS, 1), 0, blocks)
    counts = jnp.where(jnp.arange(blocks, dtype=jnp.int32)[None, None, :] == chosen, CAP, counts)
    shape = (SECTIONS, REPLICAS, blocks, TOK_DEV)
    scores = jax.random.randint(subkeys[2], shape, 0, 2 ** 20) * TOK_DEV + jnp.arange(TOK_DEV, dtype=jnp.int32)
    ranking = jnp.argsort(jnp.argsort(scores, axis=-1, stable=True), axis=-1, stable=True)
    routed = ranking < counts[..., None]
    placed = jax.random.randint(subkeys[3], shape, 0, 2)
    partner = jax.random.randint(subkeys[4], shape, 1, EXPERTS)
    offset = jax.random.randint(subkeys[5], shape, 1, EXPERTS - 1)
    second = 1 + (partner - 1 + offset) % (EXPERTS - 1)
    leading = jnp.where(routed, 0, partner)
    trailing = jnp.where(routed, partner, second)
    column_a = jnp.where(placed == 0, leading, trailing)
    column_b = jnp.where(placed == 0, trailing, leading)
    stacked = jnp.stack([column_a, column_b], axis=-1)
    return stacked.reshape(SECTIONS, REPLICAS, TOKENS, TOPK).astype(jnp.int32)


def steps_of(rng, dims, pieces, smallest, high):
    def one(dim, blocks):
        heights = jax.random.uniform(jax.random.fold_in(jax.random.fold_in(rng, 6), dim), (blocks,), jnp.float32, smallest / len(pieces), high / len(pieces))
        return jnp.repeat(jnp.exp(heights), dims[dim] // blocks).reshape((-1,) + (1,) * (len(dims) - dim - 1))

    gain = one(*pieces[0])
    for cut in pieces[1:]:
        gain = gain * one(*cut)
    return gain


def gaussian(key, dims, width, reach, pieces=(), held_as=jnp.bfloat16):
    entries = width * jax.random.normal(key, dims, jnp.float32)
    if pieces:
        entries = entries * steps_of(key, dims, pieces, -0.22, 0.18)
    return jnp.clip(entries, -reach, reach).astype(held_as)


def setup_inputs(seed: int = 0) -> dict:
    key_list = jax.random.split(jax.random.key(seed), 5)
    section_acts = gaussian(key_list[0], (SECTIONS, REPLICAS, TOKENS, D), 1.0, 6.0, ((0, 8), (1, 2), (2, 32)))
    route_ids = draw_route_ids(jax.random.fold_in(key_list[4], 71), 0)
    gate_weight = gaussian(key_list[2], (SECTIONS, D, FF), D ** -0.5, 0.109375, ((0, 8), (2, 32)))
    hidden_cot = gaussian(key_list[3], (SECTIONS, REPLICAS, SLOTS, FF), 1.0, 6.0, ((0, 8), (1, 2), (3, 32)))
    return {"section_acts": section_acts, "route_ids": route_ids, "gate_weight": gate_weight, "hidden_cot": hidden_cot}


def slot_pick(route_block, capacity):
    chosen = jnp.any(route_block == 0, axis=-1)
    ordinal = jnp.cumsum(chosen.astype(jnp.int32), axis=-1) - 1
    slot_ids = jnp.arange(capacity, dtype=jnp.int32)
    hits = (ordinal[..., None, :] == slot_ids[:, None]) & chosen[..., None, :]
    return hits.astype(jnp.float32)


def reference(section_acts, route_ids, gate_weight, hidden_cot):
    groups = TOKENS // TOK_DEV
    weight_grads = []
    input_grads = [[None] * REPLICAS for _ in range(SECTIONS)]
    for section_index in range(SECTIONS):
        weight = gate_weight[section_index]
        weight_sum = jnp.zeros((D, FF), jnp.float32)
        previous = (section_index - 1) % SECTIONS
        for replica in range(REPLICAS):
            inputs = section_acts[previous, replica].reshape(groups, TOK_DEV, D).astype(jnp.float32)
            picker = slot_pick(route_ids[section_index, replica].reshape(groups, TOK_DEV, TOPK), CAP)
            routed = jnp.einsum("gct,gtd->gcd", picker, inputs).reshape(SLOTS, D).astype(jnp.bfloat16)
            pre_act = jnp.dot(routed, weight, preferred_element_type=jnp.float32)
            sig_val = jax.nn.sigmoid(pre_act)
            pre_grad = (hidden_cot[section_index, replica].astype(jnp.float32) * sig_val * (1.0 + pre_act * (1.0 - sig_val))).astype(jnp.bfloat16)
            replica_term = jnp.dot(routed.T, pre_grad, preferred_element_type=jnp.float32).astype(jnp.bfloat16)
            weight_sum = weight_sum + replica_term.astype(jnp.float32)
            slot_grad = jnp.dot(pre_grad, weight.T, preferred_element_type=jnp.float32).astype(jnp.bfloat16)
            slot_grad = slot_grad.reshape(groups, CAP, D).astype(jnp.float32)
            spread = jnp.einsum("gct,gcd->gtd", picker, slot_grad).reshape(TOKENS, D).astype(jnp.bfloat16)
            input_grads[previous][replica] = spread
        weight_grads.append(weight_sum.astype(jnp.bfloat16))
    acts_grad = jnp.stack([jnp.stack(per_section) for per_section in input_grads])
    return (jnp.stack(weight_grads), acts_grad)
```

```python
import jax
import jax.numpy as jnp
from jax import lax
from jax.sharding import PartitionSpec as P

NY, NZ = 8, 4
K = 2


def picker_of(routes, capacity):
    chosen = jnp.any(routes == 0, axis=-1)
    tokens = chosen.shape[0]
    earlier = jnp.arange(tokens)[:, None] <= jnp.arange(tokens)[None, :]
    count = jnp.dot(
        chosen.astype(jnp.bfloat16)[None, :], earlier.astype(jnp.bfloat16), preferred_element_type=jnp.float32
    )
    slots = jnp.arange(1, capacity + 1, dtype=jnp.float32)[:, None]
    return ((count == slots) & chosen[None, :]).astype(jnp.bfloat16)


def per_device(section_acts, route_ids, gate_weight, hidden_cot):
    bf16, f32 = jnp.bfloat16, jnp.float32
    acts, routes, weight, cot = section_acts[0, 0], route_ids[0, 0], gate_weight[0], hidden_cot[0, 0]
    sections, blocks = lax.axis_size("pipe"), lax.axis_size("fsdp")
    units = weight.shape[1]
    width = weight.shape[0]
    capacity = cot.shape[0] // blocks
    f, r = lax.axis_index("fsdp"), lax.axis_index("rep")
    z = f % NZ
    columns = [[y * NZ + i for y in range(NY)] for i in range(NZ)]

    def shift(x, distance, flip=0):
        route = [
            (s * blocks + i, (s + distance) % sections * blocks + (i ^ flip))
            for s in range(sections)
            for i in range(blocks)
        ]
        return lax.ppermute(x, ("pipe", "fsdp"), route)

    def swap(x, flip):
        return lax.ppermute(x, "fsdp", [(i, i ^ flip) for i in range(blocks)])

    flips = (0, 2) if K == 2 else (0, 1, 2, 3)
    picker = picker_of(lax.ppermute(routes, "pipe", [(i, (i - 1) % sections) for i in range(sections)]), capacity)
    routed = jnp.dot(picker, acts, preferred_element_type=f32).astype(bf16)
    group = jnp.concatenate([shift(routed, 1, i) for i in flips])
    rows = lax.all_gather(group, "fsdp", axis=0, tiled=True, axis_index_groups=columns)
    cot = cot.reshape(NY, NZ, capacity, units)

    def cot_of(*zs):
        picked = [lax.dynamic_index_in_dim(cot, i, 1, keepdims=True) for i in zs]
        return jnp.concatenate(picked, axis=1).reshape(NY * len(zs) * capacity, units)

    if K == 2:
        both = jnp.concatenate([weight, swap(weight, 1)], axis=1)
        cots = jnp.concatenate([cot_of(z, z ^ 2), swap(cot_of(z ^ 1, z ^ 3), 1)], axis=1)
    else:
        both = weight
        cots = cot_of(z, z ^ 1, z ^ 2, z ^ 3)
    pre = jnp.dot(rows, both, preferred_element_type=f32)
    sig = jax.nn.sigmoid(pre)
    grad = (cots.astype(f32) * sig * (1.0 + pre * (1.0 - sig))).astype(bf16)
    slot = lax.dot_general(grad, both, (((1,), (1,)), ((), ())), preferred_element_type=f32).astype(bf16)
    part = lax.psum_scatter(slot, "fsdp", scatter_dimension=0, tiled=True, axis_index_groups=columns)
    part = part.reshape(len(flips), capacity, width)
    back = [shift(part[k], -1, i).astype(f32) for k, i in enumerate(flips)]
    slot_grad = sum(back[1:], back[0]).astype(bf16)
    acts_grad = lax.dot_general(picker, slot_grad, (((0,), (0,)), ((), ())), preferred_element_type=f32).astype(bf16)

    half = width // 2

    def term(side, block):
        chosen = lax.dynamic_slice_in_dim(rows, side * half, half, 1)
        return lax.dot_general(
            chosen, grad[:, block * units : (block + 1) * units], (((0,), (0,)), ((), ())), preferred_element_type=f32
        )

    other = 1 - r
    away, home = term(other, 0), term(r, 0)
    if K == 2:
        away = away + swap(term(other, 1).astype(bf16), 1).astype(f32)
        home = home + swap(term(r, 1).astype(bf16), 1).astype(f32)
    arrived = lax.ppermute(away.astype(bf16), "rep", [(0, 1), (1, 0)])
    weight_grad = (home.astype(bf16).astype(f32) + arrived.astype(f32)).astype(bf16)
    return weight_grad[None], acts_grad[None, None]


def solution(mesh):
    return jax.shard_map(
        per_device,
        mesh=mesh,
        in_specs=(
            P("pipe", "rep", "fsdp", None),
            P("pipe", "rep", "fsdp", None),
            P("pipe", None, "fsdp"),
            P("pipe", "rep", None, "fsdp"),
        ),
        out_specs=(P("pipe", "rep", "fsdp"), P("pipe", "rep", "fsdp", None)),
        check_vma=False,
    )
```

```python
import jax
import jax.numpy as jnp
from jax import lax
from jax.sharding import PartitionSpec as P

NY, NZ = 8, 4
K = 2


def picker_of(routes, capacity):
    chosen = jnp.any(routes == 0, axis=-1)
    tokens = chosen.shape[0]
    earlier = jnp.arange(tokens)[:, None] <= jnp.arange(tokens)[None, :]
    count = jnp.dot(
        chosen.astype(jnp.bfloat16)[None, :], earlier.astype(jnp.bfloat16), preferred_element_type=jnp.float32
    )
    slots = jnp.arange(1, capacity + 1, dtype=jnp.float32)[:, None]
    return ((count == slots) & chosen[None, :]).astype(jnp.bfloat16)


def per_device(section_acts, route_ids, gate_weight, hidden_cot):
    bf16, f32 = jnp.bfloat16, jnp.float32
    acts, routes, weight, cot = section_acts[0, 0], route_ids[0, 0], gate_weight[0], hidden_cot[0, 0]
    sections, blocks = lax.axis_size("pipe"), lax.axis_size("fsdp")
    units = weight.shape[1]
    width = weight.shape[0]
    capacity = cot.shape[0] // blocks
    f, r = lax.axis_index("fsdp"), lax.axis_index("rep")
    z = f % NZ
    columns = [[y * NZ + i for y in range(NY)] for i in range(NZ)]

    def shift(x, distance, flip=0):
        route = [
            (s * blocks + i, (s + distance) % sections * blocks + (i ^ flip))
            for s in range(sections)
            for i in range(blocks)
        ]
        return lax.ppermute(x, ("pipe", "fsdp"), route)

    def swap(x, flip):
        return lax.ppermute(x, "fsdp", [(i, i ^ flip) for i in range(blocks)])

    flips = (0, 2) if K == 2 else (0, 1, 2, 3)
    picker = picker_of(lax.ppermute(routes, "pipe", [(i, (i - 1) % sections) for i in range(sections)]), capacity)
    routed = jnp.dot(picker, acts, preferred_element_type=f32).astype(bf16)
    group = jnp.concatenate([shift(routed, 1, i) for i in flips])
    rows = lax.all_gather(group, "fsdp", axis=0, tiled=True, axis_index_groups=columns)
    cot = cot.reshape(NY, NZ, capacity, units)

    def cot_of(*zs):
        picked = [lax.dynamic_index_in_dim(cot, i, 1, keepdims=True) for i in zs]
        return jnp.concatenate(picked, axis=1).reshape(NY * len(zs) * capacity, units)

    if K == 2:
        both = jnp.concatenate([weight, swap(weight, 1)], axis=1)
        cots = jnp.concatenate([cot_of(z, z ^ 2), swap(cot_of(z ^ 1, z ^ 3), 1)], axis=1)
    else:
        both = weight
        cots = cot_of(z, z ^ 1, z ^ 2, z ^ 3)
    pre = jnp.dot(rows, both, preferred_element_type=f32)
    sig = jax.nn.sigmoid(pre)
    grad = (cots.astype(f32) * sig * (1.0 + pre * (1.0 - sig))).astype(bf16)
    half = width // 2

    def term(side, block):
        chosen = lax.dynamic_slice_in_dim(rows, side * half, half, 1)
        return lax.dot_general(
            chosen, grad[:, block * units : (block + 1) * units], (((0,), (0,)), ((), ())), preferred_element_type=f32
        )

    other = 1 - r
    first = term(other, 1).astype(bf16)
    first, grad = lax.optimization_barrier((first, grad))
    arrived_first = swap(first, 1)
    slot = lax.dot_general(grad, both, (((1,), (1,)), ((), ())), preferred_element_type=f32).astype(bf16)
    part = lax.psum_scatter(slot, "fsdp", scatter_dimension=0, tiled=True, axis_index_groups=columns)
    part = part.reshape(len(flips), capacity, width)
    back = [shift(part[k], -1, i).astype(f32) for k, i in enumerate(flips)]
    slot_grad = sum(back[1:], back[0]).astype(bf16)
    acts_grad = lax.dot_general(picker, slot_grad, (((0,), (0,)), ((), ())), preferred_element_type=f32).astype(bf16)

    away, home = term(other, 0), term(r, 0)
    if K == 2:
        away = away + arrived_first.astype(f32)
        home = home + swap(term(r, 1).astype(bf16), 1).astype(f32)
    arrived = lax.ppermute(away.astype(bf16), "rep", [(0, 1), (1, 0)])
    weight_grad = (home.astype(bf16).astype(f32) + arrived.astype(f32)).astype(bf16)
    return weight_grad[None], acts_grad[None, None]


def solution(mesh):
    return jax.shard_map(
        per_device,
        mesh=mesh,
        in_specs=(
            P("pipe", "rep", "fsdp", None),
            P("pipe", "rep", "fsdp", None),
            P("pipe", None, "fsdp"),
            P("pipe", "rep", None, "fsdp"),
        ),
        out_specs=(P("pipe", "rep", "fsdp"), P("pipe", "rep", "fsdp", None)),
        check_vma=False,
    )
```

```python
import jax
import jax.numpy as jnp
from jax import lax
from jax.sharding import PartitionSpec as P

NY, NZ = 8, 4


def picker_of(routes, capacity):
    chosen = jnp.any(routes == 0, axis=-1)
    tokens = chosen.shape[0]
    earlier = jnp.arange(tokens)[:, None] <= jnp.arange(tokens)[None, :]
    count = jnp.dot(
        chosen.astype(jnp.bfloat16)[None, :], earlier.astype(jnp.bfloat16), preferred_element_type=jnp.float32
    )
    slots = jnp.arange(1, capacity + 1, dtype=jnp.float32)[:, None]
    return ((count == slots) & chosen[None, :]).astype(jnp.bfloat16)


def per_device(section_acts, route_ids, gate_weight, hidden_cot):
    bf16, f32 = jnp.bfloat16, jnp.float32
    acts, routes, weight, cot = section_acts[0, 0], route_ids[0, 0], gate_weight[0], hidden_cot[0, 0]
    sections, blocks = lax.axis_size("pipe"), lax.axis_size("fsdp")
    units = weight.shape[1]
    width = weight.shape[0]
    capacity = cot.shape[0] // blocks
    f, r = lax.axis_index("fsdp"), lax.axis_index("rep")
    z = f % NZ
    columns = [[y * NZ + i for y in range(NY)] for i in range(NZ)]

    def shift(x, distance, flip=0):
        route = [
            (s * blocks + i, (s + distance) % sections * blocks + (i ^ flip))
            for s in range(sections)
            for i in range(blocks)
        ]
        return lax.ppermute(x, ("pipe", "fsdp"), route)

    def swap(x, flip):
        return lax.ppermute(x, "fsdp", [(i, i ^ flip) for i in range(blocks)])

    flips = (0, 2)
    picker = picker_of(lax.ppermute(routes, "pipe", [(i, (i - 1) % sections) for i in range(sections)]), capacity)
    routed = jnp.dot(picker, acts, preferred_element_type=f32).astype(bf16)
    group = jnp.concatenate([shift(routed, 1, i) for i in flips])
    rows = lax.all_gather(group, "fsdp", axis=0, tiled=True, axis_index_groups=columns)
    cot = cot.reshape(NY, NZ, capacity, units)

    def cot_of(*zs):
        picked = [lax.dynamic_index_in_dim(cot, i, 1, keepdims=True) for i in zs]
        return jnp.concatenate(picked, axis=1).reshape(NY * len(zs) * capacity, units)

    both = jnp.concatenate([weight, swap(weight, 1)], axis=1)
    cots = jnp.concatenate([cot_of(z, z ^ 2), swap(cot_of(z ^ 1, z ^ 3), 1)], axis=1)
    pre = jnp.dot(rows, both, preferred_element_type=f32)
    sig = jax.nn.sigmoid(pre)
    grad = (cots.astype(f32) * sig * (1.0 + pre * (1.0 - sig))).astype(bf16)
    half = width // 2

    def term(side, block):
        chosen = lax.dynamic_slice_in_dim(rows, side * half, half, 1)
        return lax.dot_general(
            chosen, grad[:, block * units : (block + 1) * units], (((0,), (0,)), ((), ())), preferred_element_type=f32
        )

    other = 1 - r
    first = term(other, 1).astype(bf16)
    first, grad = lax.optimization_barrier((first, grad))
    arrived_first = swap(first, 1)
    slot = lax.dot_general(grad, both, (((1,), (1,)), ((), ())), preferred_element_type=f32).astype(bf16)
    part = lax.psum_scatter(slot, "fsdp", scatter_dimension=0, tiled=True, axis_index_groups=columns)
    part = part.reshape(len(flips), capacity, width)
    back = [shift(part[k], -1, i).astype(f32) for k, i in enumerate(flips)]
    slot_grad = sum(back[1:], back[0]).astype(bf16)
    acts_grad = lax.dot_general(picker, slot_grad, (((0,), (0,)), ((), ())), preferred_element_type=f32).astype(bf16)

    arrived_second = swap(term(r, 1).astype(bf16), 1)
    away, home = lax.optimization_barrier((term(other, 0), term(r, 0)))
    arrived = lax.ppermute((away + arrived_first.astype(f32)).astype(bf16), "rep", [(0, 1), (1, 0)])
    home = lax.optimization_barrier((home + arrived_second.astype(f32)).astype(bf16))
    weight_grad = (home.astype(f32) + arrived.astype(f32)).astype(bf16)
    return weight_grad[None], acts_grad[None, None]


def solution(mesh):
    return jax.shard_map(
        per_device,
        mesh=mesh,
        in_specs=(
            P("pipe", "rep", "fsdp", None),
            P("pipe", "rep", "fsdp", None),
            P("pipe", None, "fsdp"),
            P("pipe", "rep", None, "fsdp"),
        ),
        out_specs=(P("pipe", "rep", "fsdp"), P("pipe", "rep", "fsdp", None)),
        check_vma=False,
    )
```

```python
import jax
import jax.numpy as jnp
from jax import lax
from jax.sharding import PartitionSpec as P

NY, NZ = 8, 4


def picker_of(routes, capacity):
    chosen = jnp.any(routes == 0, axis=-1)
    tokens = chosen.shape[0]
    earlier = jnp.arange(tokens)[:, None] <= jnp.arange(tokens)[None, :]
    count = jnp.dot(
        chosen.astype(jnp.bfloat16)[None, :], earlier.astype(jnp.bfloat16), preferred_element_type=jnp.float32
    )
    slots = jnp.arange(1, capacity + 1, dtype=jnp.float32)[:, None]
    return ((count == slots) & chosen[None, :]).astype(jnp.bfloat16)


def per_device(section_acts, route_ids, gate_weight, hidden_cot):
    bf16, f32 = jnp.bfloat16, jnp.float32
    acts, routes, weight, cot = section_acts[0, 0], route_ids[0, 0], gate_weight[0], hidden_cot[0, 0]
    sections, blocks = lax.axis_size("pipe"), lax.axis_size("fsdp")
    units = weight.shape[1]
    width = weight.shape[0]
    capacity = cot.shape[0] // blocks
    f, r = lax.axis_index("fsdp"), lax.axis_index("rep")
    z = f % NZ
    columns = [[y * NZ + i for y in range(NY)] for i in range(NZ)]

    def shift(x, distance, flip=0):
        route = [
            (s * blocks + i, (s + distance) % sections * blocks + (i ^ flip))
            for s in range(sections)
            for i in range(blocks)
        ]
        return lax.ppermute(x, ("pipe", "fsdp"), route)

    def swap(x, flip):
        return lax.ppermute(x, "fsdp", [(i, i ^ flip) for i in range(blocks)])

    flips = (0, 2)
    picker = picker_of(lax.ppermute(routes, "pipe", [(i, (i - 1) % sections) for i in range(sections)]), capacity)
    routed = jnp.dot(picker, acts, preferred_element_type=f32).astype(bf16)
    group = jnp.concatenate([shift(routed, 1, i) for i in flips])
    rows = lax.all_gather(group, "fsdp", axis=0, tiled=True, axis_index_groups=columns)
    cot = cot.reshape(NY, NZ, capacity, units)

    def cot_of(*zs):
        picked = [lax.dynamic_index_in_dim(cot, i, 1, keepdims=True) for i in zs]
        return jnp.concatenate(picked, axis=1).reshape(NY * len(zs) * capacity, units)

    both = jnp.concatenate([weight, swap(weight, 1)], axis=1)
    cots = jnp.concatenate([cot_of(z, z ^ 2), swap(cot_of(z ^ 1, z ^ 3), 1)], axis=1)
    pre = jnp.dot(rows, both, preferred_element_type=f32)
    sig = jax.nn.sigmoid(pre)
    grad = (cots.astype(f32) * sig * (1.0 + pre * (1.0 - sig))).astype(bf16)
    half = width // 2

    def term(side, block):
        chosen = lax.dynamic_slice_in_dim(rows, side * half, half, 1)
        return lax.dot_general(
            chosen, grad[:, block * units : (block + 1) * units], (((0,), (0,)), ((), ())), preferred_element_type=f32
        )

    other = 1 - r

    def piece(source, index):
        chosen = lax.dynamic_slice_in_dim(source, other * half + index * (half // 2), half // 2, 1)
        return lax.dot_general(
            chosen, grad[:, units:], (((0,), (0,)), ((), ())), preferred_element_type=f32
        ).astype(bf16)

    first, grad = lax.optimization_barrier((piece(rows, 0), grad))
    slot = lax.dot_general(grad, both, (((1,), (1,)), ((), ())), preferred_element_type=f32).astype(bf16)
    second = term(r, 1).astype(bf16)
    slot, second, later = lax.optimization_barrier((slot, second, rows))
    arrived_first = [swap(first, 1), swap(piece(later, 1), 1)]
    part = lax.psum_scatter(slot, "fsdp", scatter_dimension=0, tiled=True, axis_index_groups=columns)
    part = part.reshape(len(flips), capacity, width)
    back = [shift(part[k], -1, i).astype(f32) for k, i in enumerate(flips)]
    slot_grad = sum(back[1:], back[0]).astype(bf16)
    acts_grad = lax.dot_general(picker, slot_grad, (((0,), (0,)), ((), ())), preferred_element_type=f32).astype(bf16)

    arrived_second = swap(second, 1)
    away, home = lax.optimization_barrier((term(other, 0), term(r, 0)))
    kept = jnp.split(away, 2)
    lead = (kept[0] + arrived_first[0].astype(f32)).astype(bf16)
    _, came = lax.optimization_barrier((lead, arrived_first[1]))
    sent = [lead, (kept[1] + came.astype(f32)).astype(bf16)]
    arrived = jnp.concatenate([lax.ppermute(piece, "rep", [(0, 1), (1, 0)]) for piece in sent])
    home = lax.optimization_barrier((home + arrived_second.astype(f32)).astype(bf16))
    weight_grad = (home.astype(f32) + arrived.astype(f32)).astype(bf16)
    return weight_grad[None], acts_grad[None, None]


def solution(mesh):
    return jax.shard_map(
        per_device,
        mesh=mesh,
        in_specs=(
            P("pipe", "rep", "fsdp", None),
            P("pipe", "rep", "fsdp", None),
            P("pipe", None, "fsdp"),
            P("pipe", "rep", None, "fsdp"),
        ),
        out_specs=(P("pipe", "rep", "fsdp"), P("pipe", "rep", "fsdp", None)),
        check_vma=False,
    )
```
